32 devices in a mesh: groups: 2 (over x), frame: 8 (over z, y), space: 2 (over core).
Axes of the slice: x: 2, y: 2, z: 4, core: 2. Of those that a mesh axis runs over, the one named last changes fastest.
Arguments:
- queries: bfloat16 [16, 12, 80, 2240], P(('groups', 'frame'), 'space'), parts along dimension 0, may hold values from -6 to 6
- keys: bfloat16 [16, 12, 80, 2240], P(('groups', 'frame'), 'space'), parts along dimension 0, may hold values from -6 to 6
- values: bfloat16 [16, 12, 80, 2240], P(('groups', 'frame'), 'space'), parts along dimension 0, may hold values from -6 to 6
- residual: bfloat16 [16, 12, 80, 2240], P(('groups', 'frame'), 'space'), parts along dimension 0, may hold values from -6 to 6
- attn_gain: float32 [2240], replicated, may hold values from 0.5 to 1.5
- value_taps: float32 [9, 2240], replicated, may hold values from -2 to 2
- gate_taps: float32 [9, 2240], replicated, may hold values from -2 to 2
Outputs:
- block_out: bfloat16 [16, 12, 80, 2240], P(('groups', 'frame'), 'space'), parts along dimension 0
The draws below stay inside these ranges and needn't reach their ends.
There are 2 independent parts, one for each index of `groups`. The reference program is written for one: setup_inputs(seed, part) draws one part's arguments, and reference() takes and returns one part's arrays. A program takes and returns all parts, laid end to end along the dimension named above; an argument that names none is the same for every part. Nothing has to cross between parts.
All inputs are finite; a program needn't handle non-finite values.
Results may differ from the reference program's by a relative error of at most 0.008.
Values may be sent and summed in bfloat16 or wider, within the bound.
A program may use at most 128 MiB of HBM per device.

```python
import jax
import jax.numpy as jnp
from jax import lax

D = 2240
HEADS = 20
HEAD_DIM = 112
WID = 80
HGT = 12
FRAMES = 8


def block_scale(rng, shape, cuts, smallest, top_value):
    level, own = 1.0, jax.random.fold_in(rng, 6)
    for position, blocks in cuts:
        draws = jnp.exp(jax.random.uniform(jax.random.fold_in(own, position), (blocks,), jnp.float32, smallest / len(cuts), top_value / len(cuts)))
        level = level * jnp.repeat(draws, shape[position] // blocks).reshape([-1 if axis == position else 1 for axis in range(len(shape))])
    return level


def normal_values(rng, dims, deviation, limit, split=(), held_as=jnp.bfloat16):
    loudness = block_scale(rng, dims, split, -0.22, 0.18) if split else 1.0
    array = jax.random.normal(rng, dims, jnp.float32) * deviation * loudness
    return jnp.minimum(jnp.maximum(array, -limit), limit).astype(held_as)


def setup_inputs(seed: int = 0, part: int = 0) -> dict:
    key_list = jax.random.split(jax.random.key(seed), 8)
    own_keys = jax.random.split(jax.random.fold_in(key_list[7], part), 8)
    queries = normal_values(own_keys[0], (FRAMES, HGT, WID, D), 1.0, 6.0, ((0, 8), (1, 2)))
    keys = normal_values(own_keys[1], (FRAMES, HGT, WID, D), 1.0, 6.0, ((0, 8), (1, 2)))
    values = normal_values(own_keys[2], (FRAMES, HGT, WID, D), 1.0, 6.0, ((0, 8), (1, 2)))
    residual = normal_values(own_keys[3], (FRAMES, HGT, WID, D), 1.0, 6.0, ((0, 8), (1, 2)))
    attn_gain = jnp.clip(1.0 + 0.1 * jax.random.normal(key_list[4], (D,), jnp.float32), 0.5, 1.5)
    value_taps = normal_values(key_list[5], (9, D), 9 ** -0.5, 2.0, (), jnp.float32)
    gate_taps = normal_values(key_list[6], (9, D), 9 ** -0.5, 2.0, (), jnp.float32)
    return {"queries": queries, "keys": keys, "values": values, "residual": residual, "attn_gain": attn_gain, "value_taps": value_taps, "gate_taps": gate_taps}


def reference(queries, keys, values, residual, attn_gain, value_taps, gate_taps):
    tokens = HGT * WID
    feature_keys = jnp.maximum(keys, 0).reshape(FRAMES, tokens, HEADS, HEAD_DIM).astype(jnp.float32)
    value_rows = values.reshape(FRAMES, tokens, HEADS, HEAD_DIM).astype(jnp.float32)
    own_state = jnp.einsum('fthk,fthv->fhkv', feature_keys, value_rows, precision=lax.Precision.HIGHEST)
    running = jnp.cumsum(own_state, axis=0)
    prev_state = jnp.concatenate([jnp.zeros_like(own_state[:1]), running[:-1] - 0.0 * own_state[:-1]], axis=0)
    prev_state = jnp.concatenate([jnp.zeros_like(own_state[:1]), jnp.cumsum(own_state, axis=0)[:-1]], axis=0)
    previous_frame_pass = prev_state.astype(jnp.bfloat16).astype(jnp.float32)
    local_frame_pass = own_state.astype(jnp.bfloat16).astype(jnp.float32)
    feature_queries = jnp.maximum(queries, 0).reshape(FRAMES, tokens, HEADS, HEAD_DIM).astype(jnp.float32)
    numerator_sum = jnp.einsum('fthk,fhkv->fthv', feature_queries, previous_frame_pass, precision=lax.Precision.HIGHEST)
    numerator_sum = numerator_sum + jnp.einsum('fthk,fhkv->fthv', feature_queries, local_frame_pass, precision=lax.Precision.HIGHEST)
    scale = lax.rsqrt(lax.optimization_barrier(jnp.mean(numerator_sum * numerator_sum, axis=-1, keepdims=True)) + 1e-06)
    normed = (numerator_sum * scale).reshape(FRAMES, HGT, WID, D)
    mixed = (residual.astype(jnp.float32) + normed * attn_gain).astype(jnp.bfloat16)
    padded = jnp.pad(mixed.astype(jnp.float32), ((0, 0), (1, 1), (1, 1), (0, 0)))
    conv_v = jnp.zeros((FRAMES, HGT, WID, D), jnp.float32)
    conv_g = jnp.zeros((FRAMES, HGT, WID, D), jnp.float32)
    for tap_row in range(3):
        for tap_col in range(3):
            window = padded[:, tap_row:tap_row + HGT, tap_col:tap_col + WID, :]
            conv_v = conv_v + value_taps[3 * tap_row + tap_col] * window
            conv_g = conv_g + gate_taps[3 * tap_row + tap_col] * window
    block_out = mixed.astype(jnp.float32) + conv_v * jax.nn.silu(conv_g)
    return block_out.astype(jnp.bfloat16)
```

```python
import functools

import jax
import jax.numpy as jnp
from jax import lax
from jax.experimental import pallas as pl
from jax.experimental.pallas import tpu as pltpu
from jax.sharding import PartitionSpec as P

HEAD_DIM = 112
LANES = 128
WINDOW = 256
PAD = 8
F32, BF16 = jnp.float32, jnp.bfloat16


def windows(dim):
    out = []
    for lo in range(0, dim, WINDOW):
        w = min(WINDOW, dim - lo)
        h0, h1 = lo // HEAD_DIM, (lo + w - 1) // HEAD_DIM
        ks = HEAD_DIM * h0 // LANES * LANES
        ke = min(dim, -(-HEAD_DIM * (h1 + 1) // LANES) * LANES)
        out.append((lo, w, range(h0, h1 + 1), ks, ke))
    return out


def kernel(
    frames, rows, width, dim,
    q_hbm, k_hbm, v_hbm, r_hbm, gain_ref, vt_ref, gt_ref, o_hbm,
    q, k, v, res, st, pb, rb, ob, yb, pr, ps, vb, numer, sq, mixed, x32, outv,
    load_sem, rs_s, rs_r, ag_s, ag_r, y_s, y_r, z_s, z_r, pv_s, pv_r, halo_s, halo_r, out_sem,
):
    tokens = rows * width
    tiles = st.shape[0]
    per = tiles // 2
    space = lax.axis_index("space")
    frame = lax.axis_index("frame")
    other = 1 - space
    pair, odd = frame // 2, frame % 2
    twin = frame + 1 - 2 * odd
    has_prev = pair > 0
    has_next = pair < frames // 2 - 1

    loads = [
        pltpu.make_async_copy(src, dst, load_sem.at[i])
        for i, (src, dst) in enumerate(((k_hbm, k), (v_hbm, v), (q_hbm, q), (r_hbm, res)))
    ]
    for copy in loads:
        copy.start()

    barrier = pltpu.get_barrier_semaphore()
    pl.semaphore_signal(barrier, inc=1, device_id={"space": other})
    pl.semaphore_signal(barrier, inc=1, device_id={"frame": twin})

    @pl.when(has_prev)
    def _():
        pl.semaphore_signal(barrier, inc=1, device_id={"frame": frame - 2})

    @pl.when(has_next)
    def _():
        pl.semaphore_signal(barrier, inc=1, device_id={"frame": frame + 2})

    x32[...] = jnp.zeros_like(x32)
    st[tiles - 1] = jnp.zeros(st.shape[1:], F32)
    mixed[pl.ds(pl.multiple_of(space * (tokens + width), width), width), :] = jnp.zeros((width, dim), BF16)

    pl.semaphore_wait(barrier, 2 + jnp.where(has_prev, 1, 0) + jnp.where(has_next, 1, 0))

    def to_other(src, dst, tile, send, recv, j):
        return pltpu.make_async_remote_copy(
            src_ref=src.at[tile], dst_ref=dst.at[tile], send_sem=send.at[j], recv_sem=recv.at[j],
            device_id={"space": other},
        )

    def to_frame(src, dst, tile, send, recv, j, target):
        return pltpu.make_async_remote_copy(
            src_ref=src.at[tile], dst_ref=dst.at[tile], send_sem=send.at[j], recv_sem=recv.at[j],
            device_id={"frame": target},
        )

    def head_of(lo, w):
        return (lax.broadcasted_iota(jnp.int32, (HEAD_DIM, w), 1) + lo) // HEAD_DIM

    wins = windows(dim)
    loads[0].wait()
    loads[1].wait()
    order = [i // 2 if i % 2 == 0 else (len(wins) + 1) // 2 + i // 2 for i in range(len(wins))]
    for m in order:
        lo, w, heads, ks, ke = wins[m]
        full = lax.dot_general(
            jnp.maximum(k[:, ks:ke], 0), v[:, lo : lo + w], (((0,), (0,)), ((), ())), preferred_element_type=F32
        )
        owner = head_of(lo, w)
        slab = jnp.zeros((HEAD_DIM, w), F32)
        for h in heads:
            at = HEAD_DIM * h - ks
            slab = jnp.where(owner == h, full[at : at + HEAD_DIM, :], slab)
        for part in range(-(-w // LANES)):
            tile = lo // LANES + part
            wide = min(LANES, w - part * LANES)
            st[tile, :, :wide] = slab[:, part * LANES : part * LANES + wide]
            pb[tile] = st[tile].astype(BF16)

            @pl.when(other == tile // per)
            def _():
                to_other(pb, rb, tile, rs_s, rs_r, tile % per).start()

    def own_step(j, _):
        tile = space * per + j
        to_other(pb, rb, tile, rs_s, rs_r, j).wait_recv()
        total = st[tile] + rb[tile].astype(F32)
        st[tile] = total
        ob[tile] = total.astype(BF16)
        to_frame(ob, yb, tile, y_s, y_r, j, twin).start()
        to_other(ob, ob, tile, ag_s, ag_r, j).start()
        return 0

    lax.fori_loop(0, per, own_step, 0)

    def scan_step(j, _):
        tile = space * per + j
        to_frame(ob, yb, tile, y_s, y_r, j, twin).wait_recv()
        beside = yb[tile].astype(F32)

        @pl.when(has_prev)
        def _():
            to_frame(ps, pr, tile, z_s, z_r, j, frame - 2).wait_recv()

        @pl.when(jnp.logical_not(has_prev))
        def _():
            pr[tile] = jnp.zeros(pr.shape[1:], BF16)

        before = pr[tile].astype(F32)

        @pl.when(has_next)
        def _():
            ps[tile] = (before + (st[tile] + beside)).astype(BF16)
            to_frame(ps, pr, tile, z_s, z_r, j, frame + 2).start()

        vb[tile] = (before + beside * odd.astype(F32)).astype(BF16)
        to_other(vb, vb, tile, pv_s, pv_r, j).start()
        return 0

    lax.fori_loop(0, per, scan_step, 0)

    def arrive_step(j, _):
        tile = other * per + j
        to_other(ob, ob, tile, ag_s, ag_r, j).wait_recv()
        to_other(vb, vb, tile, pv_s, pv_r, j).wait_recv()
        return 0

    lax.fori_loop(0, per, arrive_step, 0)
    loads[2].wait()

    def spread(state, lo, w, heads, ks, ke):
        first = lo // LANES
        slab = jnp.concatenate([state[first + p] for p in range(-(-w // LANES))], axis=1)[:, :w]
        owner = head_of(lo, w)
        pieces = []
        if HEAD_DIM * heads[0] > ks:
            pieces.append(jnp.zeros((HEAD_DIM * heads[0] - ks, w), BF16))
        for h in heads:
            pieces.append(jnp.where(owner == h, slab, jnp.zeros_like(slab)))
        end = HEAD_DIM * (heads[-1] + 1)
        if end < ke:
            pieces.append(jnp.zeros((ke - end, w), BF16))
        return jnp.concatenate(pieces, axis=0)

    for lo, w, heads, ks, ke in wins:
        phi = jnp.maximum(q[:, ks:ke], 0)
        found = jnp.dot(phi, spread(vb, lo, w, heads, ks, ke), preferred_element_type=F32)
        found = found + jnp.dot(phi, spread(ob, lo, w, heads, ks, ke), preferred_element_type=F32)
        numer[:, lo : lo + w] = found
        sq[:, lo : lo + w] = (found * found).astype(BF16)
    loads[3].wait()
    for lo, w, heads, ks, ke in wins:
        from_head = (lax.broadcasted_iota(jnp.int32, (ke - ks, w), 0) + ks) // HEAD_DIM
        to_head = (lax.broadcasted_iota(jnp.int32, (ke - ks, w), 1) + lo) // HEAD_DIM
        same = jnp.where(from_head == to_head, 1.0, 0.0).astype(BF16)
        total = jnp.dot(sq[:, ks:ke], same, preferred_element_type=F32)
        scale = lax.rsqrt(total * (1.0 / HEAD_DIM) + 1e-6)
        normed = numer[:, lo : lo + w] * scale
        value = res[:, lo : lo + w].astype(F32) + normed * gain_ref[:, lo : lo + w]
        mixed[width : width + tokens, lo : lo + w] = value.astype(BF16)

    halo = pltpu.make_async_remote_copy(
        src_ref=mixed.at[pl.ds(pl.multiple_of(width + other * (tokens - width), width), width)],
        dst_ref=mixed.at[pl.ds(pl.multiple_of(space * (tokens + width), width), width)],
        send_sem=halo_s, recv_sem=halo_r, device_id={"space": other},
    )
    halo.start()
    halo.wait()

    step = width + 2 * PAD

    def conv(lo, w):
        at = pl.ds(lo, w)
        for row in range(rows + 2):
            x32[row * step + PAD : row * step + PAD + width, :w] = mixed[row * width : (row + 1) * width, at].astype(F32)
        for row in range(rows):
            cv = jnp.zeros((width, w), F32)
            cg = jnp.zeros((width, w), F32)
            for i in range(3):
                for j in range(3):
                    start = (row + i) * step + PAD - 1 + j
                    x = x32[start : start + width, :w]
                    cv = cv + vt_ref[3 * i + j : 3 * i + j + 1, at] * x
                    cg = cg + gt_ref[3 * i + j : 3 * i + j + 1, at] * x
            centre = (row + 1) * step + PAD
            half = 0.5 * cg
            value = x32[centre : centre + width, :w] + cv * (half + half * jnp.tanh(half))
            outv[row * width : (row + 1) * width, at] = value.astype(BF16)

    whole = dim // LANES

    def conv_step(t, _):
        conv(pl.multiple_of(t * LANES, LANES), LANES)
        return 0

    lax.fori_loop(0, whole, conv_step, 0)
    if dim % LANES:
        conv(whole * LANES, dim % LANES)
    store = pltpu.make_async_copy(outv, o_hbm, out_sem)
    store.start()

    def drain_step(j, _):
        mine, theirs = space * per + j, other * per + j
        to_other(pb, rb, theirs, rs_s, rs_r, j).wait_send()
        to_other(ob, ob, mine, ag_s, ag_r, j).wait_send()
        to_frame(ob, yb, mine, y_s, y_r, j, twin).wait_send()
        to_other(vb, vb, mine, pv_s, pv_r, j).wait_send()

        @pl.when(has_next)
        def _():
            to_frame(ps, pr, mine, z_s, z_r, j, frame + 2).wait_send()

        return 0

    lax.fori_loop(0, per, drain_step, 0)
    store.wait()


def solution(mesh):
    frames = mesh.shape["frame"]

    def on_device(queries, keys, values, residual, attn_gain, value_taps, gate_taps):
        _, rows, width, dim = queries.shape
        tokens = rows * width
        tiles = -(-dim // (2 * LANES)) * 2
        flat = lambda a: a.reshape(tokens, dim)
        anywhere = pl.BlockSpec(memory_space=pl.ANY)
        inside = pl.BlockSpec(memory_space=pltpu.VMEM)
        state = (tiles, HEAD_DIM, LANES)
        sems = pltpu.SemaphoreType.DMA((tiles // 2,))
        out = pl.pallas_call(
            functools.partial(kernel, frames, rows, width, dim),
            out_shape=jax.ShapeDtypeStruct((tokens, dim), BF16),
            in_specs=[anywhere] * 4 + [inside] * 3,
            out_specs=anywhere,
            scratch_shapes=[pltpu.VMEM((tokens, dim), BF16)] * 4
            + [pltpu.VMEM(state, F32)]
            + [pltpu.VMEM(state, BF16)] * 7
            + [
                pltpu.VMEM((tokens, dim), F32),
                pltpu.VMEM((tokens, dim), BF16),
                pltpu.VMEM((tokens + 2 * width, dim), BF16),
                pltpu.VMEM(((rows + 2) * (width + 2 * PAD), LANES), F32),
                pltpu.VMEM((tokens, dim), BF16),
                pltpu.SemaphoreType.DMA((4,)),
            ]
            + [sems] * 10
            + [pltpu.SemaphoreType.DMA] * 3,
            compiler_params=pltpu.CompilerParams(
                collective_id=0, has_side_effects=True, vmem_limit_bytes=60 << 20
            ),
        )(flat(queries), flat(keys), flat(values), flat(residual), attn_gain.reshape(1, dim), value_taps, gate_taps)
        return out.reshape(1, rows, width, dim)

    placed = P(("groups", "frame"), "space", None, None)
    return jax.shard_map(
        on_device,
        mesh=mesh,
        in_specs=(placed,) * 4 + (P(),) * 3,
        out_specs=placed,
        check_vma=False,
    )
```

```python
import functools

import jax
import jax.numpy as jnp
from jax import lax
from jax.experimental import pallas as pl
from jax.experimental.pallas import tpu as pltpu
from jax.sharding import PartitionSpec as P

HEAD_DIM = 112
LANES = 128
WINDOW = 256
PAD = 8
PIECE = 768
BLOCK = 384
LAG = 1
AHEAD = 2
F32, BF16 = jnp.float32, jnp.bfloat16


def windows(dim):
    out = []
    for lo in range(0, dim, WINDOW):
        w = min(WINDOW, dim - lo)
        h0, h1 = lo // HEAD_DIM, (lo + w - 1) // HEAD_DIM
        ks = HEAD_DIM * h0 // LANES * LANES
        ke = min(dim, -(-HEAD_DIM * (h1 + 1) // LANES) * LANES)
        out.append((lo, w, range(h0, h1 + 1), ks, ke))
    return out


def mix_kernel(
    frames, rows, width, dim,
    q_hbm, k_hbm, v_hbm, r_hbm, gain_ref, o_hbm,
    q, k, v, res, st, pb, rb, ob, yb, pr, ps, vb, numer, sq, mixed,
    kv_sem, load_sem, edge_s, edge_r, rs_s, rs_r, ag_s, ag_r, y_s, y_r, z_s, z_r, pv_s, pv_r, out_sem,
):
    tokens = rows * width
    tiles = st.shape[0]
    space = lax.axis_index("space")
    frame = lax.axis_index("frame")
    other = 1 - space
    pair, odd = frame // 2, frame % 2
    twin = frame + 1 - 2 * odd
    has_prev = pair > 0
    has_next = pair < frames // 2 - 1
    wins = windows(dim)
    steps = len(wins)

    cuts = list(range(0, dim, PIECE)) + [dim]
    kv_loads = []
    for i, (lo, hi) in enumerate(zip(cuts, cuts[1:])):
        kv_loads.append(
            [
                pltpu.make_async_copy(src.at[:, lo:hi], dst.at[:, lo:hi], kv_sem.at[c, i])
                for c, (src, dst) in enumerate(((k_hbm, k), (v_hbm, v)))
            ]
        )
    loads = [
        pltpu.make_async_copy(src, dst.at[0:tokens], load_sem.at[i]) for i, (src, dst) in enumerate(((q_hbm, q), (r_hbm, res)))
    ]
    for copies in kv_loads:
        for copy in copies:
            copy.start()
    for copy in loads:
        copy.start()

    barrier = pltpu.get_barrier_semaphore()
    pl.semaphore_signal(barrier, inc=1, device_id={"space": other})
    pl.semaphore_signal(barrier, inc=1, device_id={"frame": twin})

    @pl.when(has_prev)
    def _():
        pl.semaphore_signal(barrier, inc=1, device_id={"frame": frame - 2})

    @pl.when(has_next)
    def _():
        pl.semaphore_signal(barrier, inc=1, device_id={"frame": frame + 2})

    st[tiles - 1] = jnp.zeros(st.shape[1:], F32)
    mixed[pl.ds(pl.multiple_of(space * (tokens + width), width), width), :] = jnp.zeros((width, dim), BF16)

    pl.semaphore_wait(barrier, 2 + jnp.where(has_prev, 1, 0) + jnp.where(has_next, 1, 0))

    def to_other(src, dst, tile, send, recv, j):
        return pltpu.make_async_remote_copy(
            src_ref=src.at[tile], dst_ref=dst.at[tile], send_sem=send.at[j], recv_sem=recv.at[j],
            device_id={"space": other},
        )

    def to_frame(src, dst, tile, send, recv, j, target):
        return pltpu.make_async_remote_copy(
            src_ref=src.at[tile], dst_ref=dst.at[tile], send_sem=send.at[j], recv_sem=recv.at[j],
            device_id={"frame": target},
        )

    edges = [
        pltpu.make_async_remote_copy(
            src_ref=src.at[pl.ds(pl.multiple_of(other * (tokens - width), width), width)],
            dst_ref=dst.at[tokens : tokens + width],
            send_sem=edge_s.at[i], recv_sem=edge_r.at[i], device_id={"space": other},
        )
        for i, (src, dst) in enumerate(((q_hbm, q), (r_hbm, res)))
    ]

    def head_of(lo, w):
        return (lax.broadcasted_iota(jnp.int32, (HEAD_DIM, w), 1) + lo) // HEAD_DIM

    def own_step(j):
        tile = 2 * j + space
        to_other(pb, rb, tile, rs_s, rs_r, j).wait_recv()
        total = st[tile] + rb[tile].astype(F32)
        st[tile] = total
        ob[tile] = total.astype(BF16)
        to_frame(ob, yb, tile, y_s, y_r, j, twin).start()
        to_other(ob, ob, tile, ag_s, ag_r, j).start()

    ready = 0
    for m in range(steps):
        lo, w, heads, ks, ke = wins[m]
        while cuts[ready] < ke:
            for copy in kv_loads[ready]:
                copy.wait()
            ready += 1
        full = lax.dot_general(
            jnp.maximum(k[:, ks:ke], 0), v[:, lo : lo + w], (((0,), (0,)), ((), ())), preferred_element_type=F32
        )
        owner = head_of(lo, w)
        slab = jnp.zeros((HEAD_DIM, w), F32)
        for h in heads:
            at = HEAD_DIM * h - ks
            slab = jnp.where(owner == h, full[at : at + HEAD_DIM, :], slab)
        for part in range(-(-w // LANES)):
            tile = lo // LANES + part
            wide = min(LANES, w - part * LANES)
            st[tile, :, :wide] = slab[:, part * LANES : part * LANES + wide]
            pb[tile] = st[tile].astype(BF16)
        to_other(pb, rb, 2 * m + other, rs_s, rs_r, m).start()
        if m >= LAG:
            own_step(m - LAG)
    for m in range(max(0, steps - LAG), steps):
        own_step(m)
    for copy in edges:
        copy.start()

    def scan_step(j):
        tile = 2 * j + space
        to_frame(ob, yb, tile, y_s, y_r, j, twin).wait_recv()
        beside = yb[tile].astype(F32)

        @pl.when(has_prev)
        def _():
            to_frame(ps, pr, tile, z_s, z_r, j, frame - 2).wait_recv()

        @pl.when(jnp.logical_not(has_prev))
        def _():
            pr[tile] = jnp.zeros(pr.shape[1:], BF16)

        before = pr[tile].astype(F32)

        @pl.when(has_next)
        def _():
            ps[tile] = (before + (st[tile] + beside)).astype(BF16)
            to_frame(ps, pr, tile, z_s, z_r, j, frame + 2).start()

        vb[tile] = (before + beside * odd.astype(F32)).astype(BF16)
        to_other(vb, vb, tile, pv_s, pv_r, j).start()

    @pl.when(has_next)
    def _():
        def relay(j, _):
            scan_step(j)
            return 0

        lax.fori_loop(0, steps, relay, 0)

    def last_in_chain(first, end):
        @pl.when(jnp.logical_not(has_next))
        def _():
            for j in range(first, min(end, steps)):
                scan_step(j)

    def spread(state, lo, w, heads, ks, ke):
        first = lo // LANES
        slab = jnp.concatenate([state[first + p] for p in range(-(-w // LANES))], axis=1)[:, :w]
        owner = head_of(lo, w)
        pieces = []
        if HEAD_DIM * heads[0] > ks:
            pieces.append(jnp.zeros((HEAD_DIM * heads[0] - ks, w), BF16))
        for h in heads:
            pieces.append(jnp.where(owner == h, slab, jnp.zeros_like(slab)))
        end = HEAD_DIM * (heads[-1] + 1)
        if end < ke:
            pieces.append(jnp.zeros((ke - end, w), BF16))
        return jnp.concatenate(pieces, axis=0)

    for copy in loads:
        copy.wait()
    for copy in edges:
        copy.wait_recv()

    def numer_step(m):
        lo, w, heads, ks, ke = wins[m]
        tile = 2 * m + other
        to_other(ob, ob, tile, ag_s, ag_r, m).wait_recv()
        to_other(vb, vb, tile, pv_s, pv_r, m).wait_recv()
        phi = jnp.maximum(q[:, ks:ke], 0)
        found = jnp.dot(phi, spread(vb, lo, w, heads, ks, ke), preferred_element_type=F32)
        found = found + jnp.dot(phi, spread(ob, lo, w, heads, ks, ke), preferred_element_type=F32)
        numer[:, lo : lo + w] = found
        sq[:, lo : lo + w] = (found * found).astype(BF16)

    far = pl.ds(pl.multiple_of((1 - space) * (tokens + width), width), width)
    stores = []

    def mixed_step(m):
        lo, w, heads, ks, ke = wins[m]
        from_head = (lax.broadcasted_iota(jnp.int32, (ke - ks, w), 0) + ks) // HEAD_DIM
        to_head = (lax.broadcasted_iota(jnp.int32, (ke - ks, w), 1) + lo) // HEAD_DIM
        same = jnp.where(from_head == to_head, 1.0, 0.0).astype(BF16)
        total = jnp.dot(sq[:, ks:ke], same, preferred_element_type=F32)
        scale = lax.rsqrt(total * (1.0 / HEAD_DIM) + 1e-6)
        normed = numer[:, lo : lo + w] * scale
        value = (res[:, lo : lo + w].astype(F32) + normed * gain_ref[lo : lo + w].reshape(1, w)).astype(BF16)
        mixed[width : width + tokens, lo : lo + w] = value[:tokens]
        mixed[far, lo : lo + w] = value[tokens:]
        store = pltpu.make_async_copy(mixed.at[:, lo : lo + w], o_hbm.at[:, lo : lo + w], out_sem.at[m])
        store.start()
        stores.append(store)

    last_in_chain(0, AHEAD)
    for m in range(steps):
        last_in_chain(m + AHEAD, m + AHEAD + 1)
        numer_step(m)
        if m > 0:
            mixed_step(m - 1)
    mixed_step(steps - 1)

    for copy in edges:
        copy.wait_send()

    def drain_step(j, _):
        mine, theirs = 2 * j + space, 2 * j + other
        to_other(pb, rb, theirs, rs_s, rs_r, j).wait_send()
        to_other(ob, ob, mine, ag_s, ag_r, j).wait_send()
        to_frame(ob, yb, mine, y_s, y_r, j, twin).wait_send()
        to_other(vb, vb, mine, pv_s, pv_r, j).wait_send()

        @pl.when(has_next)
        def _():
            to_frame(ps, pr, mine, z_s, z_r, j, frame + 2).wait_send()

        return 0

    lax.fori_loop(0, steps, drain_step, 0)
    for store in stores:
        store.wait()


def conv_kernel(rows, width, m_ref, vt_ref, gt_ref, o_ref, x32):
    step = width + 2 * PAD

    @pl.when(pl.program_id(0) == 0)
    def _():
        x32[...] = jnp.zeros_like(x32)

    def tile_step(t, _):
        at = pl.ds(pl.multiple_of(t * LANES, LANES), LANES)
        for row in range(rows + 2):
            x32[row * step + PAD : row * step + PAD + width, :] = m_ref[row * width : (row + 1) * width, at].astype(F32)
        for row in range(rows):
            cv = jnp.zeros((width, LANES), F32)
            cg = jnp.zeros((width, LANES), F32)
            for i in range(3):
                for j in range(3):
                    start = (row + i) * step + PAD - 1 + j
                    x = x32[start : start + width, :]
                    cv = cv + vt_ref[3 * i + j : 3 * i + j + 1, at] * x
                    cg = cg + gt_ref[3 * i + j : 3 * i + j + 1, at] * x
            centre = (row + 1) * step + PAD
            half = 0.5 * cg
            value = x32[centre : centre + width, :] + cv * (half + half * jnp.tanh(half))
            o_ref[row * width : (row + 1) * width, at] = value.astype(BF16)
        return 0

    lax.fori_loop(0, o_ref.shape[1] // LANES, tile_step, 0)


def solution(mesh):
    frames = mesh.shape["frame"]

    def on_device(queries, keys, values, residual, attn_gain, value_taps, gate_taps):
        _, rows, width, dim = queries.shape
        tokens = rows * width
        steps = -(-dim // WINDOW)
        flat = lambda a: a.reshape(tokens, dim)
        anywhere = pl.BlockSpec(memory_space=pl.ANY)
        state = (2 * steps, HEAD_DIM, LANES)
        sems = pltpu.SemaphoreType.DMA((steps,))
        two = pltpu.SemaphoreType.DMA((2,))
        ext = tokens + width
        mixed = pl.pallas_call(
            functools.partial(mix_kernel, frames, rows, width, dim),
            out_shape=jax.ShapeDtypeStruct((tokens + 2 * width, dim), BF16),
            in_specs=[anywhere] * 4 + [pl.BlockSpec(memory_space=pltpu.VMEM)],
            out_specs=anywhere,
            scratch_shapes=[
                pltpu.VMEM((ext, dim), BF16),
                pltpu.VMEM((tokens, dim), BF16),
                pltpu.VMEM((tokens, dim), BF16),
                pltpu.VMEM((ext, dim), BF16),
                pltpu.VMEM(state, F32),
            ]
            + [pltpu.VMEM(state, BF16)] * 7
            + [
                pltpu.VMEM((ext, dim), F32),
                pltpu.VMEM((ext, dim), BF16),
                pltpu.VMEM((tokens + 2 * width, dim), BF16),
                pltpu.SemaphoreType.DMA((2, -(-dim // PIECE))),
                two,
                two,
                two,
            ]
            + [sems] * 11,
            compiler_params=pltpu.CompilerParams(collective_id=0, has_side_effects=True, vmem_limit_bytes=56 << 20),
        )(flat(queries), flat(keys), flat(values), flat(residual), attn_gain, )
        out = pl.pallas_call(
            functools.partial(conv_kernel, rows, width),
            out_shape=jax.ShapeDtypeStruct((tokens, dim), BF16),
            grid=(-(-dim // BLOCK),),
            in_specs=[
                pl.BlockSpec((tokens + 2 * width, BLOCK), lambda c: (0, c)),
                pl.BlockSpec((9, BLOCK), lambda c: (0, c)),
                pl.BlockSpec((9, BLOCK), lambda c: (0, c)),
            ],
            out_specs=pl.BlockSpec((tokens, BLOCK), lambda c: (0, c)),
            scratch_shapes=[pltpu.VMEM(((rows + 2) * (width + 2 * PAD), LANES), F32)],
        )(mixed, value_taps, gate_taps)
        return out.reshape(1, rows, width, dim)

    placed = P(("groups", "frame"), "space", None, None)
    return jax.shard_map(
        on_device,
        mesh=mesh,
        in_specs=(placed,) * 4 + (P(),) * 3,
        out_specs=placed,
        check_vma=False,
    )
```

```python
import functools

import jax
import jax.numpy as jnp
from jax import lax
from jax.experimental import pallas as pl
from jax.experimental.pallas import tpu as pltpu
from jax.sharding import PartitionSpec as P

HEAD_DIM = 112
LANES = 128
WINDOW = 256
PAD = 8
PIECE = 768
BLOCK = 384
LAG = 2
AHEAD = 2
F32, BF16 = jnp.float32, jnp.bfloat16


def windows(dim):
    out = []
    for lo in range(0, dim, WINDOW):
        w = min(WINDOW, dim - lo)
        h0, h1 = lo // HEAD_DIM, (lo + w - 1) // HEAD_DIM
        ks = HEAD_DIM * h0 // LANES * LANES
        ke = min(dim, -(-HEAD_DIM * (h1 + 1) // LANES) * LANES)
        out.append((lo, w, range(h0, h1 + 1), ks, ke))
    return out


def mix_kernel(
    frames, rows, width, dim,
    q_hbm, k_hbm, v_hbm, r_hbm, gain_ref, o_hbm,
    q, k, v, res, st, pb, rb, ob, yb, pr, ps, vb, numer, sq, mixed,
    kv_sem, load_sem, edge_s, edge_r, rs_s, rs_r, ag_s, ag_r, y_s, y_r, z_s, z_r, pv_s, pv_r, out_sem,
):
    tokens = rows * width
    tiles = st.shape[0]
    space = lax.axis_index("space")
    frame = lax.axis_index("frame")
    other = 1 - space
    pair, odd = frame // 2, frame % 2
    twin = frame + 1 - 2 * odd
    has_prev = pair > 0
    has_next = pair < frames // 2 - 1
    wins = windows(dim)
    steps = len(wins)

    cuts = list(range(0, dim, PIECE)) + [dim]
    kv_loads = []
    for i, (lo, hi) in enumerate(zip(cuts, cuts[1:])):
        kv_loads.append(
            [
                pltpu.make_async_copy(src.at[:, lo:hi], dst.at[:, lo:hi], kv_sem.at[c, i])
                for c, (src, dst) in enumerate(((k_hbm, k), (v_hbm, v)))
            ]
        )
    loads = [
        pltpu.make_async_copy(src, dst.at[0:tokens], load_sem.at[i]) for i, (src, dst) in enumerate(((q_hbm, q), (r_hbm, res)))
    ]
    for copies in kv_loads:
        for copy in copies:
            copy.start()
    for copy in loads:
        copy.start()

    barrier = pltpu.get_barrier_semaphore()
    pl.semaphore_signal(barrier, inc=1, device_id={"space": other})
    pl.semaphore_signal(barrier, inc=1, device_id={"frame": twin})

    @pl.when(has_prev)
    def _():
        pl.semaphore_signal(barrier, inc=1, device_id={"frame": frame - 2})

    @pl.when(has_next)
    def _():
        pl.semaphore_signal(barrier, inc=1, device_id={"frame": frame + 2})

    st[tiles - 1] = jnp.zeros(st.shape[1:], F32)
    mixed[pl.ds(pl.multiple_of(space * (tokens + width), width), width), :] = jnp.zeros((width, dim), BF16)

    pl.semaphore_wait(barrier, 2 + jnp.where(has_prev, 1, 0) + jnp.where(has_next, 1, 0))

    def to_other(src, dst, tile, send, recv, j):
        return pltpu.make_async_remote_copy(
            src_ref=src.at[tile], dst_ref=dst.at[tile], send_sem=send.at[j], recv_sem=recv.at[j],
            device_id={"space": other},
        )

    def to_frame(src, dst, tile, send, recv, j, target):
        return pltpu.make_async_remote_copy(
            src_ref=src.at[tile], dst_ref=dst.at[tile], send_sem=send.at[j], recv_sem=recv.at[j],
            device_id={"frame": target},
        )

    edges = [
        pltpu.make_async_remote_copy(
            src_ref=src.at[pl.ds(pl.multiple_of(other * (tokens - width), width), width)],
            dst_ref=dst.at[tokens : tokens + width],
            send_sem=edge_s.at[i], recv_sem=edge_r.at[i], device_id={"space": other},
        )
        for i, (src, dst) in enumerate(((q_hbm, q), (r_hbm, res)))
    ]

    def head_of(lo, w):
        return (lax.broadcasted_iota(jnp.int32, (HEAD_DIM, w), 1) + lo) // HEAD_DIM

    def own_step(j):
        tile = 2 * j + space
        to_other(pb, rb, tile, rs_s, rs_r, j).wait_recv()
        total = st[tile] + rb[tile].astype(F32)
        st[tile] = total
        ob[tile] = total.astype(BF16)
        to_frame(ob, yb, tile, y_s, y_r, j, twin).start()
        to_other(ob, ob, tile, ag_s, ag_r, j).start()

    ready = 0
    for m in range(steps):
        lo, w, heads, ks, ke = wins[m]
        while cuts[ready] < ke:
            for copy in kv_loads[ready]:
                copy.wait()
            ready += 1
        full = lax.dot_general(
            jnp.maximum(k[:, ks:ke], 0), v[:, lo : lo + w], (((0,), (0,)), ((), ())), preferred_element_type=F32
        )
        owner = head_of(lo, w)
        slab = jnp.zeros((HEAD_DIM, w), F32)
        for h in heads:
            at = HEAD_DIM * h - ks
            slab = jnp.where(owner == h, full[at : at + HEAD_DIM, :], slab)
        for part in range(-(-w // LANES)):
            tile = lo // LANES + part
            wide = min(LANES, w - part * LANES)
            st[tile, :, :wide] = slab[:, part * LANES : part * LANES + wide]
            pb[tile] = st[tile].astype(BF16)
        to_other(pb, rb, 2 * m + other, rs_s, rs_r, m).start()
        if m >= LAG:
            own_step(m - LAG)
    for m in range(max(0, steps - LAG), steps):
        own_step(m)
    for copy in edges:
        copy.start()

    def scan_step(j):
        tile = 2 * j + space
        to_frame(ob, yb, tile, y_s, y_r, j, twin).wait_recv()
        beside = yb[tile].astype(F32)

        @pl.when(has_prev)
        def _():
            to_frame(ps, pr, tile, z_s, z_r, j, frame - 2).wait_recv()

        @pl.when(jnp.logical_not(has_prev))
        def _():
            pr[tile] = jnp.zeros(pr.shape[1:], BF16)

        before = pr[tile].astype(F32)

        @pl.when(has_next)
        def _():
            ps[tile] = (before + (st[tile] + beside)).astype(BF16)
            to_frame(ps, pr, tile, z_s, z_r, j, frame + 2).start()

        vb[tile] = (before + beside * odd.astype(F32)).astype(BF16)
        to_other(vb, vb, tile, pv_s, pv_r, j).start()

    @pl.when(has_next)
    def _():
        def relay(j, _):
            scan_step(j)
            return 0

        lax.fori_loop(0, steps, relay, 0)

    def last_in_chain(first, end):
        @pl.when(jnp.logical_not(has_next))
        def _():
            for j in range(first, min(end, steps)):
                scan_step(j)

    def spread(state, lo, w, heads, ks, ke):
        first = lo // LANES
        slab = jnp.concatenate([state[first + p] for p in range(-(-w // LANES))], axis=1)[:, :w]
        owner = head_of(lo, w)
        pieces = []
        if HEAD_DIM * heads[0] > ks:
            pieces.append(jnp.zeros((HEAD_DIM * heads[0] - ks, w), BF16))
        for h in heads:
            pieces.append(jnp.where(owner == h, slab, jnp.zeros_like(slab)))
        end = HEAD_DIM * (heads[-1] + 1)
        if end < ke:
            pieces.append(jnp.zeros((ke - end, w), BF16))
        return jnp.concatenate(pieces, axis=0)

    for copy in loads:
        copy.wait()
    for copy in edges:
        copy.wait_recv()

    def numer_step(m):
        lo, w, heads, ks, ke = wins[m]
        tile = 2 * m + other
        to_other(ob, ob, tile, ag_s, ag_r, m).wait_recv()
        to_other(vb, vb, tile, pv_s, pv_r, m).wait_recv()
        phi = jnp.maximum(q[:, ks:ke], 0)
        found = jnp.dot(phi, spread(vb, lo, w, heads, ks, ke), preferred_element_type=F32)
        found = found + jnp.dot(phi, spread(ob, lo, w, heads, ks, ke), preferred_element_type=F32)
        numer[:, lo : lo + w] = found
        sq[:, lo : lo + w] = (found * found).astype(BF16)

    far = pl.ds(pl.multiple_of((1 - space) * (tokens + width), width), width)
    stores = []

    def mixed_step(m):
        lo, w, heads, ks, ke = wins[m]
        from_head = (lax.broadcasted_iota(jnp.int32, (ke - ks, w), 0) + ks) // HEAD_DIM
        to_head = (lax.broadcasted_iota(jnp.int32, (ke - ks, w), 1) + lo) // HEAD_DIM
        same = jnp.where(from_head == to_head, 1.0, 0.0).astype(BF16)
        total = jnp.dot(sq[:, ks:ke], same, preferred_element_type=F32)
        scale = lax.rsqrt(total * (1.0 / HEAD_DIM) + 1e-6)
        normed = numer[:, lo : lo + w] * scale
        value = (res[:, lo : lo + w].astype(F32) + normed * gain_ref[lo : lo + w].reshape(1, w)).astype(BF16)
        mixed[width : width + tokens, lo : lo + w] = value[:tokens]
        mixed[far, lo : lo + w] = value[tokens:]
        store = pltpu.make_async_copy(mixed.at[:, lo : lo + w], o_hbm.at[:, lo : lo + w], out_sem.at[m])
        store.start()
        stores.append(store)

    last_in_chain(0, AHEAD)
    for m in range(steps):
        last_in_chain(m + AHEAD, m + AHEAD + 1)
        numer_step(m)
        if m > 0:
            mixed_step(m - 1)
    mixed_step(steps - 1)

    for copy in edges:
        copy.wait_send()

    def drain_step(j, _):
        mine, theirs = 2 * j + space, 2 * j + other
        to_other(pb, rb, theirs, rs_s, rs_r, j).wait_send()
        to_other(ob, ob, mine, ag_s, ag_r, j).wait_send()
        to_frame(ob, yb, mine, y_s, y_r, j, twin).wait_send()
        to_other(vb, vb, mine, pv_s, pv_r, j).wait_send()

        @pl.when(has_next)
        def _():
            to_frame(ps, pr, mine, z_s, z_r, j, frame + 2).wait_send()

        return 0

    lax.fori_loop(0, steps, drain_step, 0)
    for store in stores:
        store.wait()


def conv_kernel(rows, width, m_ref, vt_ref, gt_ref, o_ref, x32):
    step = width + 2 * PAD
    part = 16

    @pl.when(pl.program_id(0) == 0)
    def _():
        x32[...] = jnp.zeros_like(x32)

    def tile_step(t, _):
        at = pl.ds(pl.multiple_of(t * LANES, LANES), LANES)
        for row in range(rows + 2):
            x32[row * step + PAD : row * step + PAD + width, :] = m_ref[row * width : (row + 1) * width, at].astype(F32)
        taps = [
            (jnp.broadcast_to(vt_ref[n : n + 1, at], (part, LANES)), jnp.broadcast_to(gt_ref[n : n + 1, at], (part, LANES)))
            for n in range(9)
        ]
        for row in range(rows):
            for off in range(0, width, part):
                cv, cg = None, None
                for n in range(9):
                    start = (row + n // 3) * step + PAD - 1 + n % 3 + off
                    x = x32[start : start + part, :]
                    cv = taps[n][0] * x if cv is None else cv + taps[n][0] * x
                    cg = taps[n][1] * x if cg is None else cg + taps[n][1] * x
                centre = (row + 1) * step + PAD + off
                half = 0.5 * cg
                value = x32[centre : centre + part, :] + cv * (half + half * jnp.tanh(half))
                o_ref[row * width + off : row * width + off + part, at] = value.astype(BF16)
        return 0

    lax.fori_loop(0, o_ref.shape[1] // LANES, tile_step, 0)


def solution(mesh):
    frames = mesh.shape["frame"]

    def on_device(queries, keys, values, residual, attn_gain, value_taps, gate_taps):
        _, rows, width, dim = queries.shape
        tokens = rows * width
        steps = -(-dim // WINDOW)
        flat = lambda a: a.reshape(tokens, dim)
        anywhere = pl.BlockSpec(memory_space=pl.ANY)
        state = (2 * steps, HEAD_DIM, LANES)
        sems = pltpu.SemaphoreType.DMA((steps,))
        two = pltpu.SemaphoreType.DMA((2,))
        ext = tokens + width
        mixed = pl.pallas_call(
            functools.partial(mix_kernel, frames, rows, width, dim),
            out_shape=jax.ShapeDtypeStruct((tokens + 2 * width, dim), BF16),
            in_specs=[anywhere] * 4 + [pl.BlockSpec(memory_space=pltpu.VMEM)],
            out_specs=anywhere,
            scratch_shapes=[
                pltpu.VMEM((ext, dim), BF16),
                pltpu.VMEM((tokens, dim), BF16),
                pltpu.VMEM((tokens, dim), BF16),
                pltpu.VMEM((ext, dim), BF16),
                pltpu.VMEM(state, F32),
            ]
            + [pltpu.VMEM(state, BF16)] * 7
            + [
                pltpu.VMEM((ext, dim), F32),
                pltpu.VMEM((ext, dim), BF16),
                pltpu.VMEM((tokens + 2 * width, dim), BF16),
                pltpu.SemaphoreType.DMA((2, -(-dim // PIECE))),
                two,
                two,
                two,
            ]
            + [sems] * 11,
            compiler_params=pltpu.CompilerParams(collective_id=0, has_side_effects=True, vmem_limit_bytes=56 << 20),
        )(flat(queries), flat(keys), flat(values), flat(residual), attn_gain, )
        out = pl.pallas_call(
            functools.partial(conv_kernel, rows, width),
            out_shape=jax.ShapeDtypeStruct((tokens, dim), BF16),
            grid=(-(-dim // BLOCK),),
            in_specs=[
                pl.BlockSpec((tokens + 2 * width, BLOCK), lambda c: (0, c)),
                pl.BlockSpec((9, BLOCK), lambda c: (0, c)),
                pl.BlockSpec((9, BLOCK), lambda c: (0, c)),
            ],
            out_specs=pl.BlockSpec((tokens, BLOCK), lambda c: (0, c)),
            scratch_shapes=[pltpu.VMEM(((rows + 2) * (width + 2 * PAD), LANES), F32)],
        )(mixed, value_taps, gate_taps)
        return out.reshape(1, rows, width, dim)

    placed = P(("groups", "frame"), "space", None, None)
    return jax.shard_map(
        on_device,
        mesh=mesh,
        in_specs=(placed,) * 4 + (P(),) * 3,
        out_specs=placed,
        check_vma=False,
    )
```
